32 devices in a mesh: obs: 8 (over z, core), state: 4 (over y, x).
Axes of the slice: x: 2, y: 2, z: 4, core: 2. Of those that a mesh axis runs over, the one named last changes fastest.
Arguments:
- ensemble: bfloat16 [4, 1024, 256], P('state'), may hold values from -16 to 16
- obs_values: float32 [16384], P('obs'), may hold values from -72 to 72
- obs_error: float32 [16384], P('obs'), may hold values from 6 to 24
- h_blocks: bfloat16 [8, 4, 64, 128, 128], P('obs', 'state'), may hold values from -0.125 to 0.125
- block_rows: int32 [8, 4, 64], P('obs', 'state'), may hold values from 0 to 15
- block_cols: int32 [8, 4, 64], P('obs', 'state'), may hold values from 0 to 7
- block_count: int32 [8, 4], P('obs', 'state'), may hold values from 32 to 64, as said below
Outputs:
- analysis: bfloat16 [4, 1024, 256], P('state', 'obs')
The draws below stay inside these ranges and needn't reach their ends.
Inputs may be any that keep to these rules, and one draw needn't show every extreme that they name: `block_count`: some device has exactly 64 live slots in every draw.
All inputs are finite; a program needn't handle non-finite values.
Results may differ from the reference program's by a relative error of at most 0.009.
Values sent between devices are 32-bit elements; how exact they have to be, the bound alone decides.
A program may use at most 64 MiB of HBM per device.

```python
import math
import jax
import jax.numpy as jnp
from jax import lax

K = 256
BS = 128
M_DEV = 2048
BLK_DEV = 64
OBLK = 16
SLAB = 1024
OBS = 16384
N_OBS = 8
N_STATE = 4


def draw_ensemble(key, part):
    first_key, second_key, third_key = jax.random.split(jax.random.fold_in(key, 11), 3)
    normals = jax.random.normal(first_key, (N_STATE * SLAB, K), jnp.float32)
    mixing = jax.random.normal(second_key, (K, K), jnp.float32) / jnp.sqrt(jnp.float32(K))
    members = normals + 0.6 * jnp.dot(normals, mixing)
    scales = jnp.exp(jax.random.uniform(third_key, (K,), jnp.float32, jnp.log(0.5), jnp.log(2.0)))
    members = members * scales[None, :]
    members = jnp.clip(members, -16.0, 16.0)
    return members.reshape(N_STATE, SLAB, K).astype(jnp.bfloat16)


def draw_block_count(key, part):
    counts = jax.random.randint(jax.random.fold_in(key, 21), (N_OBS * N_STATE,), BLK_DEV // 2, BLK_DEV + 1)
    chosen = jax.random.randint(jax.random.fold_in(key, 22), (), 0, N_OBS * N_STATE)
    counts = jnp.where(jnp.arange(N_OBS * N_STATE) == chosen, BLK_DEV, counts)
    return counts.reshape(N_OBS, N_STATE).astype(jnp.int32)


def set_ends(values, own_key, smallest, top_value):
    longest = values.shape.index(max(values.shape))
    spots = []
    for shift in (0, 1):
        where = [jax.random.randint(jax.random.fold_in(own_key, axis), (), 0, length) for axis, length in enumerate(values.shape)]
        where[longest] = (where[longest] + shift) % values.shape[longest]
        spots.append(tuple(where))
    return values.at[spots[0]].set(smallest).at[spots[1]].set(top_value)


def level_of(key, shape, cuts, smallest, top_value):
    def one(axis_at, parts):
        steps = jax.random.uniform(jax.random.fold_in(jax.random.fold_in(key, 6), axis_at), (parts,), jnp.float32, smallest / len(cuts), top_value / len(cuts))
        return jnp.repeat(jnp.exp(steps), shape[axis_at] // parts).reshape((-1,) + (1,) * (len(shape) - axis_at - 1))

    factor_of = one(*cuts[0])
    for cut in cuts[1:]:
        factor_of = factor_of * one(*cut)
    return factor_of


def scatter_about(stream_key, shape, scale, reach, shards=(), kind=jnp.bfloat16):
    drawn = jax.random.normal(stream_key, shape, jnp.float32) * scale
    if len(shards) > 0:
        drawn = level_of(stream_key, shape, shards, -0.22, 0.18) * drawn
    return jnp.clip(drawn, min=-reach, max=reach).astype(kind)


def setup_inputs(seed: int = 0) -> dict:
    keys = jax.random.split(jax.random.key(seed), 8)
    ensemble = draw_ensemble(jax.random.fold_in(keys[7], 71), 0)
    obs_values = scatter_about(keys[1], (OBS,), 12.0, 72.0, ((0, 8),), jnp.float32)
    obs_error = jnp.clip(jnp.exp(math.log(24.0) - 1.3862944 * jax.random.uniform(keys[2], (OBS,), jnp.float32) ** level_of(keys[2], (OBS,), ((0, 8),), -0.2, 0.2)), 6.0, 24.0)
    h_blocks = scatter_about(keys[3], (N_OBS, N_STATE, BLK_DEV, BS, BS), (BLK_DEV * BS * N_STATE // OBLK) ** -0.5, 0.125, ((0, 8), (1, 4)))
    block_rows = set_ends(jax.random.randint(keys[4], (N_OBS, N_STATE, BLK_DEV), 0, OBLK), jax.random.fold_in(keys[4], 1), 0, OBLK - 1).astype(jnp.int32)
    block_cols = set_ends(jax.random.randint(keys[5], (N_OBS, N_STATE, BLK_DEV), 0, SLAB // BS), jax.random.fold_in(keys[5], 1), 0, (SLAB // BS) - 1).astype(jnp.int32)
    block_count = draw_block_count(jax.random.fold_in(keys[7], 71), 0)
    return dict(ensemble=ensemble, obs_values=obs_values, obs_error=obs_error, h_blocks=h_blocks, block_rows=block_rows, block_cols=block_cols, block_count=block_count)


def apply_blocks(members, blocks, rows_index, cols_index, count_live):
    state_blocks = members.shape[0] // BS
    picked = members.reshape(state_blocks, BS, K)[cols_index].astype(jnp.float32)
    products = jnp.einsum('bij,bjk->bik', blocks.astype(jnp.float32), picked)
    live_mask = jnp.arange(BLK_DEV) < count_live
    onehot = ((rows_index[None, :] == jnp.arange(OBLK)[:, None]) & live_mask[None, :]).astype(jnp.float32)
    summed = jnp.einsum('mb,bik->mik', onehot, products, precision=lax.Precision.HIGHEST)
    return summed.reshape(M_DEV, K)

def reference(ensemble, obs_values, obs_error, h_blocks, block_rows, block_cols, block_count):

    def per_shard(obs_index):

        def add_slab(carry, state_index):
            contrib = apply_blocks(ensemble[state_index], h_blocks[obs_index, state_index], block_rows[obs_index, state_index], block_cols[obs_index, state_index], block_count[obs_index, state_index])
            return (carry + contrib, state_index)
        summed, unused = lax.scan(add_slab, jnp.zeros((M_DEV, K), jnp.float32), jnp.arange(N_STATE))
        return summed
    projected = lax.map(per_shard, jnp.arange(N_OBS)).reshape(OBS, K)
    obs_mean = lax.optimization_barrier(jnp.mean(projected, axis=1))
    whitened = (projected - obs_mean[:, None]) / obs_error[:, None]
    innovation = (obs_values - obs_mean) / obs_error
    identity = jnp.eye(K, dtype=jnp.float32)
    precision = (K - 1) * identity + jnp.dot(whitened.T, whitened, precision=lax.Precision.HIGHEST)
    projected_innovation = jnp.dot(innovation, whitened, precision=lax.Precision.HIGHEST)
    lower_factor = jnp.linalg.cholesky(precision)
    halfway = lax.linalg.triangular_solve(lower_factor, projected_innovation[:, None], left_side=True, lower=True)
    mean_weight = lax.linalg.triangular_solve(lower_factor, halfway, left_side=True, lower=True, transpose_a=True)
    root_inverse = lax.linalg.triangular_solve(lower_factor, identity, left_side=True, lower=True, transpose_a=True)
    transform = (math.sqrt(K - 1) * root_inverse + mean_weight).astype(jnp.bfloat16)
    widened = ensemble.astype(jnp.float32)
    state_mean = lax.optimization_barrier(jnp.mean(widened, axis=2))
    anomalies = (widened - state_mean[:, :, None]).astype(jnp.bfloat16)
    moved = jnp.dot(anomalies.reshape(N_STATE * SLAB, K).astype(jnp.float32), transform.astype(jnp.float32), preferred_element_type=jnp.float32)
    analysis = state_mean[:, :, None] + moved.reshape(N_STATE, SLAB, K)
    return analysis.astype(jnp.bfloat16)
```

```python
import functools
import math

import jax
import jax.numpy as jnp
from jax import lax
from jax.experimental import pallas as pl
from jax.experimental.pallas import tpu as pltpu
from jax.sharding import PartitionSpec as P

LANES = 128
MESH = pl.DeviceIdType.MESH
VMEM = pl.BlockSpec(memory_space=pltpu.VMEM)
SMEM = pl.BlockSpec(memory_space=pltpu.SMEM)
ANY = pl.BlockSpec(memory_space=pl.ANY)
HIGHEST = lax.Precision.HIGHEST


def project_kernel(groups, rows_ref, cols_ref, count_ref, members_hbm, blocks_hbm, out_ref, members, blocks, sems):
    slots = blocks.shape[0]
    per = slots // groups
    spare = out_ref.shape[1] - 1
    load_members = pltpu.make_async_copy(members_hbm, members, sems.at[groups])
    load_members.start()
    loads = []
    for g in range(groups):
        part = pl.ds(g * per, per)
        loads.append(pltpu.make_async_copy(blocks_hbm.at[part], blocks.at[part], sems.at[g]))
        loads[-1].start()
    out_ref[...] = jnp.zeros_like(out_ref)
    live = count_ref[0, 0]
    load_members.wait()
    for g in range(groups):
        loads[g].wait()

        def add_some(step, carry, g=g):
            base = g * per + step * 4
            products = []
            for k in range(4):
                products.append(
                    jnp.dot(blocks[base + k], members[cols_ref[0, base + k]], preferred_element_type=jnp.float32)
                )
            for k in range(4):
                slot = base + k
                row = jnp.where(slot < live, rows_ref[0, slot], spare)
                out_ref[0, row] += products[k][:, :LANES]
                out_ref[1, row] += products[k][:, LANES:]
            return carry

        lax.fori_loop(0, per // 4, add_some, 0)


def project(members, blocks, rows, cols, count, obs_blocks):
    slots, size, unused = blocks.shape
    width = members.shape[-1]
    groups = 4
    return pl.pallas_call(
        functools.partial(project_kernel, groups),
        out_shape=jax.ShapeDtypeStruct((2, obs_blocks + 1, size, width // 2), jnp.float32),
        in_specs=[SMEM, SMEM, SMEM, ANY, ANY],
        out_specs=VMEM,
        scratch_shapes=[
            pltpu.VMEM(members.shape, members.dtype),
            pltpu.VMEM(blocks.shape, blocks.dtype),
            pltpu.SemaphoreType.DMA((groups + 1,)),
        ],
        name="project",
    )(rows, cols, count, members, blocks)


def stage_plan(bits, order):
    plan = []
    for at, bit in enumerate(order):
        later = order[at + 1:]
        kept = [0]
        for other in later:
            kept = kept + [rel | (1 << other) for rel in kept]
        kept = sorted(kept, key=lambda rel: [-((rel >> other) & 1) for other in later])
        plan.append((bit, kept))
    return plan


def columns_of(row):
    return jnp.transpose(jnp.broadcast_to(row, (LANES, LANES)))


def combine_kernel(n_obs, n_state, terms, values_ref, errors_ref, out_ref, got0, got1, errs, innov, white, gram, part_in, mine, z_in, full, send, recv, send_b, recv_b):
    state = lax.axis_index("state")
    obs = lax.axis_index("obs")
    core = obs % 2
    z = obs // 2
    n_z = n_obs // 2
    bits = int(math.log2(n_state))
    group = n_state * 2
    share = white.shape[0]
    members = white.shape[1]
    per = share // LANES

    def flipped(rel):
        total = 0
        for bit in range(bits):
            own = (state // (1 << bit)) % 2
            total = total + (1 << bit) * ((own + ((rel >> bit) & 1)) % 2)
        return total

    peers = []
    for shift in range(1, group):
        index = (state * 2 + core + shift) % group
        peers.append((z * 2 + index % 2, index // 2))
    z_peers = [(((z + shift) % n_z) * 2 + core, state) for shift in range(1, n_z)]

    barrier = pltpu.get_barrier_semaphore()
    for peer in peers + z_peers:
        pl.semaphore_signal(barrier, inc=1, device_id=peer, device_id_type=MESH)
    pl.semaphore_wait(barrier, len(peers) + len(z_peers))

    def piece(half, index):
        return terms.at[half, pl.ds(index * per, per)]

    got = (got0, got1)
    plans = (stage_plan(bits, list(range(bits))), stage_plan(bits, list(range(bits))[::-1]))
    slot_of = []
    for plan in plans:
        slots = {}
        for at, (bit, kept) in enumerate(plan):
            for rel in kept:
                slots[at, rel] = len(slots)
        slot_of.append(slots)
    copies = {}

    def launch(half, at, rel):
        bit = plans[half][at][0]
        sent_rel = rel | (1 << bit)
        if at == 0:
            source = piece(half, flipped(sent_rel))
        else:
            source = got[half].at[slot_of[half][at - 1, sent_rel]]
        slot = slot_of[half][at, rel]
        copy = pltpu.make_async_remote_copy(
            src_ref=source,
            dst_ref=got[half].at[slot],
            send_sem=send.at[half, slot],
            recv_sem=recv.at[half, slot],
            device_id=(obs, flipped(1 << bit)),
            device_id_type=MESH,
        )
        copy.start()
        copies[half, at, rel] = copy

    for index in range(len(plans[0][0][1])):
        for half in range(2):
            launch(half, 0, plans[half][0][1][index])
    for k in range(per):
        at_rows = pl.ds(k * LANES, LANES)
        errs[at_rows] = columns_of(errors_ref[pl.ds(state * per + k, 1), :])
        innov[at_rows] = columns_of(values_ref[pl.ds(state * per + k, 1), :])
    for at in range(bits):
        for index in range(len(plans[0][at][1])):
            for half in range(2):
                rel = plans[half][at][1][index]
                copies[half, at, rel].wait_recv()
                slot = slot_of[half][at, rel]
                if at == 0:
                    got[half][slot] += terms[half, pl.ds(flipped(rel) * per, per)]
                else:
                    got[half][slot] += got[half][slot_of[half][at - 1, rel]]
                if at + 1 < bits and (rel >> plans[half][at + 1][0]) & 1:
                    launch(half, at + 1, rel ^ (1 << plans[half][at + 1][0]))
    last = [slot_of[half][bits - 1, 0] for half in range(2)]
    low, high = [got[half][last[half]].reshape(share, LANES) for half in range(2)]
    mean = (jnp.sum(low, axis=1, keepdims=True) + jnp.sum(high, axis=1, keepdims=True)) / members
    white[:, :LANES] = (low - mean) / errs[...]
    white[:, LANES:] = (high - mean) / errs[...]
    weight = (innov[...] - mean) / errs[...]
    whole = white[...]
    gram[...] = lax.dot_general(
        whole, whole, (((0,), (0,)), ((), ())), precision=HIGHEST, preferred_element_type=jnp.float32
    )
    gram[0:1, LANES:] = jnp.sum(whole[:, :LANES] * weight, axis=0, keepdims=True)
    gram[1:2, LANES:] = jnp.sum(whole[:, LANES:] * weight, axis=0, keepdims=True)

    own = state * 2 + core
    rows = members // group

    def rows_of(index):
        return pl.ds(index * rows, rows)

    def send_to(source, target, at, peer):
        copy = pltpu.make_async_remote_copy(
            src_ref=source,
            dst_ref=target,
            send_sem=send_b.at[at],
            recv_sem=recv_b.at[at],
            device_id=peer,
            device_id_type=MESH,
        )
        copy.start()
        return copy

    first = []
    for k, peer in enumerate(peers):
        index = (own + k + 1) % group
        first.append(send_to(gram.at[rows_of(index)], part_in.at[k], k, peer))
    total = gram[rows_of(own), :]
    for k, copy in enumerate(first):
        copy.wait_recv()
        total = total + part_in[k]
    mine[...] = total
    second = []
    for k, peer in enumerate(z_peers):
        second.append(send_to(mine, z_in.at[k], group - 1 + k, peer))
    for k, copy in enumerate(second):
        copy.wait_recv()
        total = total + z_in[k]
    full[rows_of(own), :] = total
    third = []
    for k, peer in enumerate(peers):
        third.append(send_to(full.at[rows_of(own)], full.at[rows_of(own)], group - 1 + n_z - 1 + k, peer))
    for copy in third:
        copy.wait_recv()
    out_ref[...] = full[...]
    for copy in list(copies.values()) + first + second + third:
        copy.wait_send()


def combine(terms, values, errors, n_obs, n_state, obs_blocks):
    size = terms.shape[2]
    members = 2 * terms.shape[3]
    per = obs_blocks // n_state
    group = 2 * n_state
    n_z = n_obs // 2
    count = n_state - 1
    others = 2 * (group - 1) + n_z - 1
    return pl.pallas_call(
        functools.partial(combine_kernel, n_obs, n_state),
        out_shape=jax.ShapeDtypeStruct((members, members), jnp.float32),
        in_specs=[VMEM] * 3,
        out_specs=VMEM,
        scratch_shapes=[
            pltpu.VMEM((count, per, size, members // 2), jnp.float32),
            pltpu.VMEM((count, per, size, members // 2), jnp.float32),
            pltpu.VMEM((per * size, LANES), jnp.float32),
            pltpu.VMEM((per * size, LANES), jnp.float32),
            pltpu.VMEM((per * size, members), jnp.float32),
            pltpu.VMEM((members, members), jnp.float32),
            pltpu.VMEM((group - 1, members // group, members), jnp.float32),
            pltpu.VMEM((members // group, members), jnp.float32),
            pltpu.VMEM((n_z - 1, members // group, members), jnp.float32),
            pltpu.VMEM((members, members), jnp.float32),
            pltpu.SemaphoreType.DMA((2, count)),
            pltpu.SemaphoreType.DMA((2, count)),
            pltpu.SemaphoreType.DMA((others,)),
            pltpu.SemaphoreType.DMA((others,)),
        ],
        compiler_params=pltpu.CompilerParams(collective_id=0, has_side_effects=True),
        name="combine",
    )(terms, values, errors)


def three_parts(x):
    first = x.astype(jnp.bfloat16)
    rest = x - first.astype(jnp.float32)
    second = rest.astype(jnp.bfloat16)
    third = (rest - second.astype(jnp.float32)).astype(jnp.bfloat16)
    return first, second, third


def inverse_factor(work):
    size = work.shape[0]
    step = 8
    lane = lax.broadcasted_iota(jnp.int32, (step, LANES), 1)
    sub = lax.broadcasted_iota(jnp.int32, (step, LANES), 0)
    row_of = lax.broadcasted_iota(jnp.int32, (size, 1), 0)

    def panel(at, carry):
        start = pl.multiple_of(at * step, step)
        left = work[pl.ds(start, step), :LANES]
        right = work[pl.ds(start, step), LANES:]
        cols = [
            jnp.broadcast_to(jnp.sum(jnp.where(lane == start + k, left, 0.0), axis=1, keepdims=True), (step, LANES))
            for k in range(step)
        ]
        for k in range(step):
            scale = lax.rsqrt(jnp.broadcast_to(cols[k][k:k + 1, :], (step, LANES)))
            factor = cols[k] * scale
            below = sub > k

            def eliminate(x):
                row = jnp.broadcast_to(x[k:k + 1, :], (step, LANES)) * scale
                return jnp.where(below, x - factor * row, jnp.where(sub == k, row, x))

            left = eliminate(left)
            right = eliminate(right)
            for m in range(k + 1, step):
                cols[m] = eliminate(cols[m])
        work[pl.ds(start, step), :LANES] = left
        work[pl.ds(start, step), LANES:] = right
        first, second, third = three_parts(left)
        wide = jnp.concatenate([left, right], axis=1)
        one, two, three = three_parts(wide)
        lhs = jnp.concatenate([first, first, second, second, first, third], axis=0)
        rhs = jnp.concatenate([one, two, one, two, three, one], axis=0)
        change = lax.dot_general(lhs, rhs, (((0,), (0,)), ((), ())), preferred_element_type=jnp.float32)
        work[...] = jnp.where(row_of >= start + step, work[...] - change, work[...])
        return carry

    lax.fori_loop(0, size // step, panel, 0)


def dot_exact(a, b, dims):
    return lax.dot_general(a, b, (dims, ((), ())), precision=HIGHEST, preferred_element_type=jnp.float32)


def analyse_kernel(prior, sums, members_hbm, out_ref, piece, first, second, factor, sem):
    rows, members = piece.shape
    load = pltpu.make_async_copy(members_hbm.at[pl.ds(lax.axis_index("obs") * rows, rows)], piece, sem)
    load.start()
    row_at = lax.broadcasted_iota(jnp.int32, (LANES, LANES), 0)
    col_at = lax.broadcasted_iota(jnp.int32, (LANES, LANES), 1)
    eye = jnp.where(row_at == col_at, 1.0, 0.0).astype(jnp.float32)
    first[:, :LANES] = sums[:LANES, :LANES] + prior * eye
    first[:, LANES:] = eye
    inverse_factor(first)
    upper = first[:, LANES:]
    across = dot_exact(sums[LANES:, :LANES], upper, ((1,), (1,)))
    second[:, :LANES] = sums[LANES:, LANES:] + prior * eye - dot_exact(across, across, ((1,), (1,)))
    second[:, LANES:] = eye
    inverse_factor(second)
    lower = second[:, LANES:]
    factor[:LANES, :LANES] = upper
    factor[:LANES, LANES:] = jnp.zeros_like(eye)
    factor[LANES:, LANES:] = lower
    factor[LANES:, :LANES] = -dot_exact(lower, dot_exact(across, upper, ((1,), (0,))), ((1,), (0,)))
    inverse = factor[...]
    moved = jnp.concatenate([sums[0:1, LANES:], sums[1:2, LANES:]], axis=1)
    halfway = jnp.sum(inverse * moved, axis=1, keepdims=True)
    mean_weight = jnp.sum(inverse * halfway, axis=0, keepdims=True)
    transform = (math.sqrt(prior) * inverse + mean_weight).astype(jnp.bfloat16)
    load.wait()
    widened = piece[...].astype(jnp.float32)
    state_mean = jnp.mean(widened, axis=1, keepdims=True)
    anomalies = (widened - state_mean).astype(jnp.bfloat16)
    change = lax.dot_general(anomalies, transform, (((1,), (1,)), ((), ())), preferred_element_type=jnp.float32)
    out_ref[...] = (state_mean + change).astype(jnp.bfloat16)


def analyse(sums, members, n_obs):
    slab_rows, width = members.shape
    rows = slab_rows // n_obs
    return pl.pallas_call(
        functools.partial(analyse_kernel, float(width - 1)),
        out_shape=jax.ShapeDtypeStruct((rows, width), jnp.bfloat16),
        in_specs=[VMEM, ANY],
        out_specs=VMEM,
        scratch_shapes=[
            pltpu.VMEM((rows, width), jnp.bfloat16),
            pltpu.VMEM((LANES, 2 * LANES), jnp.float32),
            pltpu.VMEM((LANES, 2 * LANES), jnp.float32),
            pltpu.VMEM((width, width), jnp.float32),
            pltpu.SemaphoreType.DMA,
        ],
        name="analyse",
    )(sums, members)


def on_device(n_obs, n_state, ensemble, obs_values, obs_error, h_blocks, block_rows, block_cols, block_count):
    members = ensemble[0]
    slab_rows, width = members.shape
    size = h_blocks.shape[-1]
    obs_blocks = obs_values.shape[0] // size
    terms = project(
        members.reshape(slab_rows // size, size, width),
        h_blocks[0, 0],
        block_rows[0],
        block_cols[0],
        block_count,
        obs_blocks,
    )
    sums = combine(
        terms,
        obs_values.reshape(obs_blocks, size),
        obs_error.reshape(obs_blocks, size),
        n_obs,
        n_state,
        obs_blocks,
    )
    return analyse(sums, members, n_obs)[None]


def solution(mesh):
    placed = (
        P("state", None, None),
        P("obs"),
        P("obs"),
        P("obs", "state", None, None, None),
        P("obs", "state", None),
        P("obs", "state", None),
        P("obs", "state"),
    )
    return jax.shard_map(
        functools.partial(on_device, mesh.shape["obs"], mesh.shape["state"]),
        mesh=mesh,
        in_specs=placed,
        out_specs=P("state", "obs", None),
        check_vma=False,
    )
```

```python
import functools
import math

import jax
import jax.numpy as jnp
from jax import lax
from jax.experimental import pallas as pl
from jax.experimental.pallas import tpu as pltpu
from jax.sharding import PartitionSpec as P

LANES = 128
SUBLANES = 8
BLOCKS = ((0, 0), (1, 0), (1, 1))
MESH = pl.DeviceIdType.MESH
VMEM = pl.BlockSpec(memory_space=pltpu.VMEM)
SMEM = pl.BlockSpec(memory_space=pltpu.SMEM)
ANY = pl.BlockSpec(memory_space=pl.ANY)
HIGHEST = lax.Precision.HIGHEST


def project_kernel(groups, rows_ref, cols_ref, count_ref, members_hbm, blocks_hbm, out_ref, members, blocks, sems):
    slots = blocks.shape[0]
    per = slots // groups
    together = math.gcd(per, 16)
    spare = out_ref.shape[1] - 1
    load_members = pltpu.make_async_copy(members_hbm, members, sems.at[groups])
    load_members.start()
    loads = []
    for g in range(groups):
        part = pl.ds(g * per, per)
        loads.append(pltpu.make_async_copy(blocks_hbm.at[part], blocks.at[part], sems.at[g]))
        loads[-1].start()
    out_ref[...] = jnp.zeros_like(out_ref)
    live = count_ref[0, 0]
    load_members.wait()
    for g in range(groups):
        loads[g].wait()

        def add_some(step, carry, g=g):
            base = g * per + step * together
            products = []
            for k in range(together):
                products.append(
                    jnp.dot(blocks[base + k], members[cols_ref[0, base + k]], preferred_element_type=jnp.float32)
                )
            for k in range(together):
                slot = base + k
                row = jnp.where(slot < live, rows_ref[0, slot], spare)
                out_ref[0, row] += products[k][:, :LANES]
                out_ref[1, row] += products[k][:, LANES:]
            return carry

        lax.fori_loop(0, per // together, add_some, 0)


def project(members, blocks, rows, cols, count, obs_blocks):
    slots, size, unused = blocks.shape
    width = members.shape[-1]
    groups = 4
    return pl.pallas_call(
        functools.partial(project_kernel, groups),
        out_shape=pltpu.VMEM((2, obs_blocks + 1, size, width // 2), jnp.float32),
        in_specs=[SMEM, SMEM, SMEM, ANY, ANY],
        out_specs=VMEM,
        scratch_shapes=[
            pltpu.VMEM(members.shape, members.dtype),
            pltpu.VMEM(blocks.shape, blocks.dtype),
            pltpu.SemaphoreType.DMA((groups + 1,)),
        ],
        name="project",
    )(rows, cols, count, members, blocks)


def stage_plan(bits, order):
    plan = []
    for at, bit in enumerate(order):
        later = order[at + 1:]
        kept = [0]
        for other in later:
            kept = kept + [rel | (1 << other) for rel in kept]
        kept = sorted(kept, key=lambda rel: [-((rel >> other) & 1) for other in later])
        plan.append((bit, kept))
    return plan


def half_turn(row):
    return jnp.concatenate([row[:, LANES // 2:], row[:, :LANES // 2]], axis=1)


def columns_of(row):
    return jnp.transpose(jnp.broadcast_to(row, (LANES, LANES)))


def combine_kernel(n_obs, n_state, terms, values_ref, errors_ref, out_ref, got0, got1, errs, innov, gram, part_in, mine, z_in, full, send, recv, send_b, recv_b):
    state = lax.axis_index("state")
    obs = lax.axis_index("obs")
    core = obs % 2
    z = obs // 2
    n_z = n_obs // 2
    bits = int(math.log2(n_state))
    group = n_state * 2
    share = errs.shape[0]
    members = 2 * terms.shape[3]
    per = share // LANES

    def flipped(rel):
        total = 0
        for bit in range(bits):
            own = (state // (1 << bit)) % 2
            total = total + (1 << bit) * ((own + ((rel >> bit) & 1)) % 2)
        return total

    peers = []
    for shift in range(1, group):
        index = (state * 2 + core + shift) % group
        peers.append((z * 2 + index % 2, index // 2))
    z_peers = [(((z + shift) % n_z) * 2 + core, state) for shift in range(1, n_z)]

    barrier = pltpu.get_barrier_semaphore()
    for peer in peers + z_peers:
        pl.semaphore_signal(barrier, inc=1, device_id=peer, device_id_type=MESH)
    pl.semaphore_wait(barrier, len(peers) + len(z_peers))

    def piece(half, index):
        return terms.at[half, pl.ds(index * per, per)]

    got = (got0, got1)
    plans = (stage_plan(bits, list(range(bits))), stage_plan(bits, list(range(bits))[::-1]))
    slot_of = []
    for plan in plans:
        slots = {}
        for at, (bit, kept) in enumerate(plan):
            for rel in kept:
                slots[at, rel] = len(slots)
        slot_of.append(slots)
    copies = {}

    def launch(half, at, rel):
        bit = plans[half][at][0]
        sent_rel = rel | (1 << bit)
        if at == 0:
            source = piece(half, flipped(sent_rel))
        else:
            source = got[half].at[slot_of[half][at - 1, sent_rel]]
        slot = slot_of[half][at, rel]
        copy = pltpu.make_async_remote_copy(
            src_ref=source,
            dst_ref=got[half].at[slot],
            send_sem=send.at[half, slot],
            recv_sem=recv.at[half, slot],
            device_id=(obs, flipped(1 << bit)),
            device_id_type=MESH,
        )
        copy.start()
        copies[half, at, rel] = copy

    for index in range(len(plans[0][0][1])):
        for half in range(2):
            launch(half, 0, plans[half][0][1][index])
    for k in range(per):
        at_rows = pl.ds(k * LANES, LANES)
        errs[at_rows] = 1.0 / columns_of(errors_ref[pl.ds(state * per + k, 1), :])
        innov[at_rows] = columns_of(values_ref[pl.ds(state * per + k, 1), :])
    for at in range(bits):
        for index in range(len(plans[0][at][1])):
            for half in range(2):
                rel = plans[half][at][1][index]
                copies[half, at, rel].wait_recv()
                slot = slot_of[half][at, rel]
                if at == 0:
                    got[half][slot] += terms[half, pl.ds(flipped(rel) * per, per)]
                else:
                    got[half][slot] += got[half][slot_of[half][at - 1, rel]]
                if at + 1 < bits and (rel >> plans[half][at + 1][0]) & 1:
                    launch(half, at + 1, rel ^ (1 << plans[half][at + 1][0]))
    last = [slot_of[half][bits - 1, 0] for half in range(2)]
    low, high = [got[half][last[half]].reshape(share, LANES) for half in range(2)]
    mean = (jnp.sum(low, axis=1, keepdims=True) + jnp.sum(high, axis=1, keepdims=True)) / members
    low = (low - mean) * errs[...]
    high = (high - mean) * errs[...]
    weight = (innov[...] - mean) * errs[...]
    sum_low = jnp.sum(low * weight, axis=0, keepdims=True)
    sum_high = jnp.sum(high * weight, axis=0, keepdims=True)
    whole = jnp.concatenate([low, high], axis=1)
    upper = whole.astype(jnp.bfloat16)
    rest = (whole - upper.astype(jnp.float32)).astype(jnp.bfloat16)
    turned = jnp.transpose(upper)
    square = jnp.dot(turned, upper, preferred_element_type=jnp.float32)
    cross = jnp.dot(turned, rest, preferred_element_type=jnp.float32)
    tiles = LANES // SUBLANES
    for k, (i, j) in enumerate(BLOCKS):
        block_i, block_j = slice(i * LANES, (i + 1) * LANES), slice(j * LANES, (j + 1) * LANES)
        block = square[block_i, block_j] + (cross[block_i, block_j] + jnp.transpose(cross[block_j, block_i]))
        gram[k * tiles:(k + 1) * tiles] = block.reshape(tiles, SUBLANES, LANES)
    lane = lax.broadcasted_iota(jnp.int32, (1, LANES), 1)
    for k, row in enumerate([sum_low, half_turn(sum_low), sum_high, half_turn(sum_high)]):
        at = SUBLANES - 4 + k
        gram[tiles - 1, at:at + 1, :] = jnp.where(lane < LANES // 2, row, gram[tiles - 1, at:at + 1, :])
    if gram.shape[0] > len(BLOCKS) * tiles:
        gram[len(BLOCKS) * tiles:] = jnp.zeros_like(gram[len(BLOCKS) * tiles:])

    own = state * 2 + core
    rows = gram.shape[0] // group

    def rows_of(index):
        return pl.ds(index * rows, rows)

    def send_to(source, target, at, peer):
        copy = pltpu.make_async_remote_copy(
            src_ref=source,
            dst_ref=target,
            send_sem=send_b.at[at],
            recv_sem=recv_b.at[at],
            device_id=peer,
            device_id_type=MESH,
        )
        copy.start()
        return copy

    first = []
    for k, peer in enumerate(peers):
        index = (own + k + 1) % group
        first.append(send_to(gram.at[rows_of(index)], part_in.at[k], k, peer))
    total = gram[rows_of(own)]
    for k, copy in enumerate(first):
        copy.wait_recv()
        total = total + part_in[k]
    mine[...] = total
    second = []
    for k, peer in enumerate(z_peers):
        second.append(send_to(mine, z_in.at[k], group - 1 + k, peer))
    for k, copy in enumerate(second):
        copy.wait_recv()
        total = total + z_in[k]
    full[rows_of(own)] = total
    third = []
    for k, peer in enumerate(peers):
        third.append(send_to(full.at[rows_of(own)], full.at[rows_of(own)], group - 1 + n_z - 1 + k, peer))
    for copy in third:
        copy.wait_recv()
    out_ref[...] = full[...]
    for copy in list(copies.values()) + first + second + third:
        copy.wait_send()


def combine(terms, values, errors, n_obs, n_state, obs_blocks):
    size = terms.shape[2]
    members = 2 * terms.shape[3]
    per = obs_blocks // n_state
    group = 2 * n_state
    n_z = n_obs // 2
    count = n_state - 1
    tiles = group * pl.cdiv(len(BLOCKS) * LANES // SUBLANES, group)
    others = 2 * (group - 1) + n_z - 1
    return pl.pallas_call(
        functools.partial(combine_kernel, n_obs, n_state),
        out_shape=pltpu.VMEM((tiles, SUBLANES, LANES), jnp.float32),
        in_specs=[VMEM] * 3,
        out_specs=VMEM,
        scratch_shapes=[
            pltpu.VMEM((count, per, size, members // 2), jnp.float32),
            pltpu.VMEM((count, per, size, members // 2), jnp.float32),
            pltpu.VMEM((per * size, LANES), jnp.float32),
            pltpu.VMEM((per * size, LANES), jnp.float32),
            pltpu.VMEM((tiles, SUBLANES, LANES), jnp.float32),
            pltpu.VMEM((group - 1, tiles // group, SUBLANES, LANES), jnp.float32),
            pltpu.VMEM((tiles // group, SUBLANES, LANES), jnp.float32),
            pltpu.VMEM((n_z - 1, tiles // group, SUBLANES, LANES), jnp.float32),
            pltpu.VMEM((tiles, SUBLANES, LANES), jnp.float32),
            pltpu.SemaphoreType.DMA((2, count)),
            pltpu.SemaphoreType.DMA((2, count)),
            pltpu.SemaphoreType.DMA((others,)),
            pltpu.SemaphoreType.DMA((others,)),
        ],
        compiler_params=pltpu.CompilerParams(collective_id=0, has_side_effects=True),
        name="combine",
    )(pltpu.with_memory_space_constraint(terms, pltpu.VMEM), values, errors)


def three_parts(x):
    first = x.astype(jnp.bfloat16)
    rest = x - first.astype(jnp.float32)
    second = rest.astype(jnp.bfloat16)
    third = (rest - second.astype(jnp.float32)).astype(jnp.bfloat16)
    return first, second, third


def inverse_factor(work):
    size = work.shape[0]
    step = 16
    lane = lax.broadcasted_iota(jnp.int32, (step, LANES), 1)
    sub = lax.broadcasted_iota(jnp.int32, (step, LANES), 0)
    row_of = lax.broadcasted_iota(jnp.int32, (size, 1), 0)

    def panel(at, carry):
        start = pl.multiple_of(at * step, step)
        left = work[pl.ds(start, step), :LANES]
        right = work[pl.ds(start, step), LANES:]
        cols = [
            jnp.broadcast_to(jnp.sum(jnp.where(lane == start + k, left, 0.0), axis=1, keepdims=True), (step, LANES))
            for k in range(step)
        ]
        for k in range(step):
            scale = lax.rsqrt(jnp.broadcast_to(cols[k][k:k + 1, :], (step, LANES)))
            factor = cols[k] * scale
            below = sub > k

            def eliminate(x):
                row = jnp.broadcast_to(x[k:k + 1, :], (step, LANES)) * scale
                return jnp.where(below, x - factor * row, jnp.where(sub == k, row, x))

            left = eliminate(left)
            right = eliminate(right)
            for m in range(k + 1, step):
                cols[m] = eliminate(cols[m])
        work[pl.ds(start, step), :LANES] = left
        work[pl.ds(start, step), LANES:] = right
        first, second, third = three_parts(left)
        wide = jnp.concatenate([left, right], axis=1)
        one, two, three = three_parts(wide)
        lhs = jnp.concatenate([first, first, second, second, first, third], axis=0)
        rhs = jnp.concatenate([one, two, one, two, three, one], axis=0)
        change = lax.dot_general(lhs, rhs, (((0,), (0,)), ((), ())), preferred_element_type=jnp.float32)
        work[...] = jnp.where(row_of >= start + step, work[...] - change, work[...])
        return carry

    lax.fori_loop(0, size // step, panel, 0)


def dot_exact(a, b, dims):
    return lax.dot_general(a, b, (dims, ((), ())), precision=HIGHEST, preferred_element_type=jnp.float32)


def analyse_kernel(prior, sums, members_hbm, out_ref, piece, first, second, factor, sem):
    rows, members = piece.shape
    load = pltpu.make_async_copy(members_hbm.at[pl.ds(lax.axis_index("obs") * rows, rows)], piece, sem)
    load.start()
    row_at = lax.broadcasted_iota(jnp.int32, (LANES, LANES), 0)
    col_at = lax.broadcasted_iota(jnp.int32, (LANES, LANES), 1)
    tiles = LANES // SUBLANES
    corner, side, other = [sums[k * tiles:(k + 1) * tiles].reshape(LANES, LANES) for k in range(len(BLOCKS))]
    eye = jnp.where(row_at == col_at, 1.0, 0.0).astype(jnp.float32)
    first[:, :LANES] = corner + prior * eye
    first[:, LANES:] = eye
    inverse_factor(first)
    upper = first[:, LANES:]
    across = dot_exact(side, upper, ((1,), (1,)))
    second[:, :LANES] = other + prior * eye - dot_exact(across, across, ((1,), (1,)))
    second[:, LANES:] = eye
    inverse_factor(second)
    lower = second[:, LANES:]
    factor[:LANES, :LANES] = upper
    factor[:LANES, LANES:] = jnp.zeros_like(eye)
    factor[LANES:, LANES:] = lower
    factor[LANES:, :LANES] = -dot_exact(lower, dot_exact(across, upper, ((1,), (0,))), ((1,), (0,)))
    inverse = factor[...]
    lane = lax.broadcasted_iota(jnp.int32, (1, LANES), 1)
    parts = [corner[LANES - 4 + k:LANES - 3 + k, :] for k in range(4)]
    moved = jnp.concatenate(
        [jnp.where(lane < LANES // 2, parts[k], half_turn(parts[k + 1])) for k in (0, 2)], axis=1
    )
    halfway = jnp.sum(inverse * moved, axis=1, keepdims=True)
    mean_weight = jnp.sum(inverse * halfway, axis=0, keepdims=True)
    transform = (math.sqrt(prior) * inverse + mean_weight).astype(jnp.bfloat16)
    load.wait()
    widened = piece[...].astype(jnp.float32)
    state_mean = jnp.mean(widened, axis=1, keepdims=True)
    anomalies = (widened - state_mean).astype(jnp.bfloat16)
    change = lax.dot_general(anomalies, transform, (((1,), (1,)), ((), ())), preferred_element_type=jnp.float32)
    out_ref[...] = (state_mean + change).astype(jnp.bfloat16)


def analyse(sums, members, n_obs):
    slab_rows, width = members.shape
    rows = slab_rows // n_obs
    return pl.pallas_call(
        functools.partial(analyse_kernel, float(width - 1)),
        out_shape=jax.ShapeDtypeStruct((rows, width), jnp.bfloat16),
        in_specs=[VMEM, ANY],
        out_specs=VMEM,
        scratch_shapes=[
            pltpu.VMEM((rows, width), jnp.bfloat16),
            pltpu.VMEM((LANES, 2 * LANES), jnp.float32),
            pltpu.VMEM((LANES, 2 * LANES), jnp.float32),
            pltpu.VMEM((width, width), jnp.float32),
            pltpu.SemaphoreType.DMA,
        ],
        name="analyse",
    )(pltpu.with_memory_space_constraint(sums, pltpu.VMEM), members)


def on_device(n_obs, n_state, ensemble, obs_values, obs_error, h_blocks, block_rows, block_cols, block_count):
    members = ensemble[0]
    slab_rows, width = members.shape
    size = h_blocks.shape[-1]
    obs_blocks = obs_values.shape[0] // size
    terms = project(
        members.reshape(slab_rows // size, size, width),
        h_blocks[0, 0],
        block_rows[0],
        block_cols[0],
        block_count,
        obs_blocks,
    )
    sums = combine(
        terms,
        obs_values.reshape(obs_blocks, size),
        obs_error.reshape(obs_blocks, size),
        n_obs,
        n_state,
        obs_blocks,
    )
    return analyse(sums, members, n_obs)[None]


def solution(mesh):
    placed = (
        P("state", None, None),
        P("obs"),
        P("obs"),
        P("obs", "state", None, None, None),
        P("obs", "state", None),
        P("obs", "state", None),
        P("obs", "state"),
    )
    return jax.shard_map(
        functools.partial(on_device, mesh.shape["obs"], mesh.shape["state"]),
        mesh=mesh,
        in_specs=placed,
        out_specs=P("state", "obs", None),
        check_vma=False,
    )
```

```python
import functools
import math

import jax
import jax.numpy as jnp
from jax import lax
from jax.experimental import pallas as pl
from jax.experimental.pallas import tpu as pltpu
from jax.sharding import PartitionSpec as P

LANES = 128
SUBLANES = 8
BLOCKS = ((0, 0), (1, 0), (1, 1))
MESH = pl.DeviceIdType.MESH
VMEM = pl.BlockSpec(memory_space=pltpu.VMEM)
SMEM = pl.BlockSpec(memory_space=pltpu.SMEM)
ANY = pl.BlockSpec(memory_space=pl.ANY)
HIGHEST = lax.Precision.HIGHEST


def sort_slots(rows_row, live, obs_blocks, out):
    slots = rows_row.shape[1]
    at_row = lax.broadcasted_iota(jnp.int32, (1, slots), 1)
    key_row = jnp.where(at_row < live, rows_row, obs_blocks).astype(jnp.float32)
    sub = lax.broadcasted_iota(jnp.int32, (slots, slots), 0)
    lane = lax.broadcasted_iota(jnp.int32, (slots, slots), 1)
    keys = jnp.broadcast_to(key_row, (slots, slots))
    key_col = jnp.sum(jnp.where(sub == lane, keys, 0.0), axis=1, keepdims=True)
    ahead = (keys < key_col) | ((keys == key_col) & (lane < sub))
    rank = jnp.sum(jnp.where(ahead, 1.0, 0.0), axis=1, keepdims=True)
    place = lax.broadcasted_iota(jnp.int32, (slots, LANES), 1).astype(jnp.float32)
    slot = lax.broadcasted_iota(jnp.int32, (slots, LANES), 0).astype(jnp.float32)
    chosen = rank == place
    order = jnp.sum(jnp.where(chosen, slot, 0.0), axis=0, keepdims=True)
    sorted_key = jnp.sum(jnp.where(chosen, key_col, 0.0), axis=0, keepdims=True)
    smaller = jnp.sum(jnp.where(key_col < sorted_key, 1.0, 0.0), axis=0, keepdims=True)
    same = jnp.where(smaller == place[0:1], 0.0, 1.0)
    upto = jnp.sum(jnp.where(key_col <= place, 1.0, 0.0), axis=0, keepdims=True)
    present = jnp.sum(jnp.where(key_col == place, 1.0, 0.0), axis=0, keepdims=True)
    last = jnp.maximum(upto - 1.0, 0.0)
    out[0:1, :] = order.astype(jnp.int32)
    out[1:2, :] = same.astype(jnp.int32)
    out[2:3, :] = last.astype(jnp.int32)
    out[3:4, :] = jnp.minimum(present, 1.0).astype(jnp.int32)
    out[4:, :] = jnp.zeros_like(out[4:, :])


def project_half(half, lists, cols_ref, members, blocks, running, terms):
    slots = blocks.shape[0]
    together = math.gcd(slots, 16)

    def add_some(step, total):
        base = step * together
        products = []
        for k in range(together):
            slot = jnp.clip(lists[0, base + k], 0, slots - 1)
            picked = members[cols_ref[0, slot], :, half * LANES:(half + 1) * LANES]
            products.append(jnp.dot(blocks[slot], picked, preferred_element_type=jnp.float32))
        for k in range(together):
            total = total * lists[1, base + k].astype(jnp.float32) + products[k]
            running[base + k] = total
        return total

    lax.fori_loop(0, slots // together, add_some, jnp.zeros(running.shape[1:], jnp.float32))
    for row in range(terms.shape[1]):
        terms[half, row] = running[jnp.clip(lists[2, row], 0, slots - 1)] * lists[3, row].astype(jnp.float32)


def stage_plan(bits, order):
    plan = []
    for at, bit in enumerate(order):
        later = order[at + 1:]
        kept = [0]
        for other in later:
            kept = kept + [rel | (1 << other) for rel in kept]
        kept = sorted(kept, key=lambda rel: [-((rel >> other) & 1) for other in later])
        plan.append((bit, kept))
    return plan


def half_turn(row):
    return jnp.concatenate([row[:, LANES // 2:], row[:, :LANES // 2]], axis=1)


def columns_of(row):
    return jnp.transpose(jnp.broadcast_to(row, (LANES, LANES)))


def combine_kernel(n_obs, n_state, count_ref, cols_ref, rows_ref, members_hbm, blocks_hbm, values_ref, errors_ref, out_ref, members_in, blocks, sorted_in, lists, running, terms, loads, got0, got1, errs, innov, gram, part_in, mine, z_in, full, send, recv, send_b, recv_b):
    load_members = pltpu.make_async_copy(members_hbm, members_in, loads.at[0])
    load_blocks = pltpu.make_async_copy(blocks_hbm, blocks, loads.at[1])
    load_members.start()
    load_blocks.start()
    state = lax.axis_index("state")
    obs = lax.axis_index("obs")
    core = obs % 2
    z = obs // 2
    n_z = n_obs // 2
    bits = int(math.log2(n_state))
    group = n_state * 2
    share = errs.shape[0]
    members = 2 * terms.shape[3]
    per = share // LANES

    def flipped(rel):
        total = 0
        for bit in range(bits):
            own = (state // (1 << bit)) % 2
            total = total + (1 << bit) * ((own + ((rel >> bit) & 1)) % 2)
        return total

    peers = []
    for shift in range(1, group):
        index = (state * 2 + core + shift) % group
        peers.append((z * 2 + index % 2, index // 2))
    z_peers = [(((z + shift) % n_z) * 2 + core, state) for shift in range(1, n_z)]

    barrier = pltpu.get_barrier_semaphore()
    for peer in peers + z_peers:
        pl.semaphore_signal(barrier, inc=1, device_id=peer, device_id_type=MESH)
    sort_slots(rows_ref[...], count_ref[0, 0], terms.shape[1], sorted_in)
    load_lists = pltpu.make_async_copy(sorted_in, lists, loads.at[2])
    load_lists.start()
    load_lists.wait()
    load_members.wait()
    load_blocks.wait()
    project_half(0, lists, cols_ref, members_in, blocks, running, terms)
    pl.semaphore_wait(barrier, len(peers) + len(z_peers))

    def piece(half, index):
        return terms.at[half, pl.ds(index * per, per)]

    got = (got0, got1)
    plans = (stage_plan(bits, list(range(bits))), stage_plan(bits, list(range(bits))[::-1]))
    slot_of = []
    for plan in plans:
        slots = {}
        for at, (bit, kept) in enumerate(plan):
            for rel in kept:
                slots[at, rel] = len(slots)
        slot_of.append(slots)
    copies = {}

    def launch(half, at, rel):
        bit = plans[half][at][0]
        sent_rel = rel | (1 << bit)
        if at == 0:
            source = piece(half, flipped(sent_rel))
        else:
            source = got[half].at[slot_of[half][at - 1, sent_rel]]
        slot = slot_of[half][at, rel]
        copy = pltpu.make_async_remote_copy(
            src_ref=source,
            dst_ref=got[half].at[slot],
            send_sem=send.at[half, slot],
            recv_sem=recv.at[half, slot],
            device_id=(obs, flipped(1 << bit)),
            device_id_type=MESH,
        )
        copy.start()
        copies[half, at, rel] = copy

    for half in range(2):
        if half == 1:
            project_half(1, lists, cols_ref, members_in, blocks, running, terms)
        for rel in plans[half][0][1]:
            launch(half, 0, rel)
    for k in range(per):
        at_rows = pl.ds(k * LANES, LANES)
        errs[at_rows] = 1.0 / columns_of(errors_ref[pl.ds(state * per + k, 1), :])
        innov[at_rows] = columns_of(values_ref[pl.ds(state * per + k, 1), :])
    for at in range(bits):
        for index in range(len(plans[0][at][1])):
            for half in range(2):
                rel = plans[half][at][1][index]
                copies[half, at, rel].wait_recv()
                slot = slot_of[half][at, rel]
                if at == 0:
                    got[half][slot] += terms[half, pl.ds(flipped(rel) * per, per)]
                else:
                    got[half][slot] += got[half][slot_of[half][at - 1, rel]]
                if at + 1 < bits and (rel >> plans[half][at + 1][0]) & 1:
                    launch(half, at + 1, rel ^ (1 << plans[half][at + 1][0]))
    last = [slot_of[half][bits - 1, 0] for half in range(2)]
    low, high = [got[half][last[half]].reshape(share, LANES) for half in range(2)]
    mean = (jnp.sum(low, axis=1, keepdims=True) + jnp.sum(high, axis=1, keepdims=True)) / members
    low = (low - mean) * errs[...]
    high = (high - mean) * errs[...]
    weight = (innov[...] - mean) * errs[...]
    sum_low = jnp.sum(low * weight, axis=0, keepdims=True)
    sum_high = jnp.sum(high * weight, axis=0, keepdims=True)
    whole = jnp.concatenate([low, high], axis=1)
    upper = whole.astype(jnp.bfloat16)
    rest = (whole - upper.astype(jnp.float32)).astype(jnp.bfloat16)
    turned = jnp.transpose(upper)
    square = jnp.dot(turned, upper, preferred_element_type=jnp.float32)
    cross = jnp.dot(turned, rest, preferred_element_type=jnp.float32)
    tiles = LANES // SUBLANES
    for k, (i, j) in enumerate(BLOCKS):
        block_i, block_j = slice(i * LANES, (i + 1) * LANES), slice(j * LANES, (j + 1) * LANES)
        block = square[block_i, block_j] + (cross[block_i, block_j] + jnp.transpose(cross[block_j, block_i]))
        gram[k * tiles:(k + 1) * tiles] = block.reshape(tiles, SUBLANES, LANES)
    lane = lax.broadcasted_iota(jnp.int32, (1, LANES), 1)
    for k, row in enumerate([sum_low, half_turn(sum_low), sum_high, half_turn(sum_high)]):
        at = SUBLANES - 4 + k
        gram[tiles - 1, at:at + 1, :] = jnp.where(lane < LANES // 2, row, gram[tiles - 1, at:at + 1, :])
    if gram.shape[0] > len(BLOCKS) * tiles:
        gram[len(BLOCKS) * tiles:] = jnp.zeros_like(gram[len(BLOCKS) * tiles:])

    own = state * 2 + core
    rows = gram.shape[0] // group

    def rows_of(index):
        return pl.ds(index * rows, rows)

    def send_to(source, target, at, peer):
        copy = pltpu.make_async_remote_copy(
            src_ref=source,
            dst_ref=target,
            send_sem=send_b.at[at],
            recv_sem=recv_b.at[at],
            device_id=peer,
            device_id_type=MESH,
        )
        copy.start()
        return copy

    first = []
    for k, peer in enumerate(peers):
        index = (own + k + 1) % group
        first.append(send_to(gram.at[rows_of(index)], part_in.at[k], k, peer))
    total = gram[rows_of(own)]
    for k, copy in enumerate(first):
        copy.wait_recv()
        total = total + part_in[k]
    mine[...] = total
    second = []
    for k, peer in enumerate(z_peers):
        second.append(send_to(mine, z_in.at[k], group - 1 + k, peer))
    for k, copy in enumerate(second):
        copy.wait_recv()
        total = total + z_in[k]
    full[rows_of(own)] = total
    third = []
    for k, peer in enumerate(peers):
        third.append(send_to(full.at[rows_of(own)], full.at[rows_of(own)], group - 1 + n_z - 1 + k, peer))
    for copy in third:
        copy.wait_recv()
    out_ref[...] = full[...]
    for copy in list(copies.values()) + first + second + third:
        copy.wait_send()


def combine(members, blocks, rows, cols, count, values, errors, n_obs, n_state, obs_blocks):
    slots, size, unused = blocks.shape
    width = members.shape[-1]
    per = obs_blocks // n_state
    group = 2 * n_state
    n_z = n_obs // 2
    pieces = n_state - 1
    tiles = group * pl.cdiv(len(BLOCKS) * LANES // SUBLANES, group)
    others = 2 * (group - 1) + n_z - 1
    return pl.pallas_call(
        functools.partial(combine_kernel, n_obs, n_state),
        out_shape=pltpu.VMEM((tiles, SUBLANES, LANES), jnp.float32),
        in_specs=[SMEM, SMEM, VMEM, ANY, ANY, VMEM, VMEM],
        out_specs=VMEM,
        scratch_shapes=[
            pltpu.VMEM(members.shape, members.dtype),
            pltpu.VMEM(blocks.shape, blocks.dtype),
            pltpu.VMEM((SUBLANES, LANES), jnp.int32),
            pltpu.SMEM((SUBLANES, LANES), jnp.int32),
            pltpu.VMEM((slots, size, width // 2), jnp.float32),
            pltpu.VMEM((2, obs_blocks, size, width // 2), jnp.float32),
            pltpu.SemaphoreType.DMA((3,)),
            pltpu.VMEM((pieces, per, size, width // 2), jnp.float32),
            pltpu.VMEM((pieces, per, size, width // 2), jnp.float32),
            pltpu.VMEM((per * size, LANES), jnp.float32),
            pltpu.VMEM((per * size, LANES), jnp.float32),
            pltpu.VMEM((tiles, SUBLANES, LANES), jnp.float32),
            pltpu.VMEM((group - 1, tiles // group, SUBLANES, LANES), jnp.float32),
            pltpu.VMEM((tiles // group, SUBLANES, LANES), jnp.float32),
            pltpu.VMEM((n_z - 1, tiles // group, SUBLANES, LANES), jnp.float32),
            pltpu.VMEM((tiles, SUBLANES, LANES), jnp.float32),
            pltpu.SemaphoreType.DMA((2, pieces)),
            pltpu.SemaphoreType.DMA((2, pieces)),
            pltpu.SemaphoreType.DMA((others,)),
            pltpu.SemaphoreType.DMA((others,)),
        ],
        compiler_params=pltpu.CompilerParams(collective_id=0, has_side_effects=True),
        name="combine",
    )(count, cols, rows, members, blocks, values, errors)


def three_parts(x):
    first = x.astype(jnp.bfloat16)
    rest = x - first.astype(jnp.float32)
    second = rest.astype(jnp.bfloat16)
    third = (rest - second.astype(jnp.float32)).astype(jnp.bfloat16)
    return first, second, third


def inverse_factor(work):
    size = work.shape[0]
    step = 16
    lane = lax.broadcasted_iota(jnp.int32, (step, LANES), 1)
    sub = lax.broadcasted_iota(jnp.int32, (step, LANES), 0)
    row_of = lax.broadcasted_iota(jnp.int32, (size, 1), 0)

    def panel(at, carry):
        start = pl.multiple_of(at * step, step)
        left = work[pl.ds(start, step), :LANES]
        right = work[pl.ds(start, step), LANES:]
        cols = [
            jnp.broadcast_to(jnp.sum(jnp.where(lane == start + k, left, 0.0), axis=1, keepdims=True), (step, LANES))
            for k in range(step)
        ]
        for k in range(step):
            scale = lax.rsqrt(jnp.broadcast_to(cols[k][k:k + 1, :], (step, LANES)))
            factor = cols[k] * scale
            below = sub > k

            def eliminate(x):
                row = jnp.broadcast_to(x[k:k + 1, :], (step, LANES)) * scale
                return jnp.where(below, x - factor * row, jnp.where(sub == k, row, x))

            left = eliminate(left)
            right = eliminate(right)
            for m in range(k + 1, step):
                cols[m] = eliminate(cols[m])
        work[pl.ds(start, step), :LANES] = left
        work[pl.ds(start, step), LANES:] = right
        first, second, third = three_parts(left)
        wide = jnp.concatenate([left, right], axis=1)
        one, two, three = three_parts(wide)
        lhs = jnp.concatenate([first, first, second, second, first, third], axis=0)
        rhs = jnp.concatenate([one, two, one, two, three, one], axis=0)
        change = lax.dot_general(lhs, rhs, (((0,), (0,)), ((), ())), preferred_element_type=jnp.float32)
        work[...] = jnp.where(row_of >= start + step, work[...] - change, work[...])
        return carry

    lax.fori_loop(0, size // step, panel, 0)


def dot_exact(a, b, dims):
    return lax.dot_general(a, b, (dims, ((), ())), precision=HIGHEST, preferred_element_type=jnp.float32)


def analyse_kernel(prior, sums, members_hbm, out_ref, piece, first, second, factor, sem):
    rows, members = piece.shape
    load = pltpu.make_async_copy(members_hbm.at[pl.ds(lax.axis_index("obs") * rows, rows)], piece, sem)
    load.start()
    row_at = lax.broadcasted_iota(jnp.int32, (LANES, LANES), 0)
    col_at = lax.broadcasted_iota(jnp.int32, (LANES, LANES), 1)
    tiles = LANES // SUBLANES
    corner, side, other = [sums[k * tiles:(k + 1) * tiles].reshape(LANES, LANES) for k in range(len(BLOCKS))]
    eye = jnp.where(row_at == col_at, 1.0, 0.0).astype(jnp.float32)
    first[:, :LANES] = corner + prior * eye
    first[:, LANES:] = eye
    inverse_factor(first)
    upper = first[:, LANES:]
    across = dot_exact(side, upper, ((1,), (1,)))
    second[:, :LANES] = other + prior * eye - dot_exact(across, across, ((1,), (1,)))
    second[:, LANES:] = eye
    inverse_factor(second)
    lower = second[:, LANES:]
    factor[:LANES, :LANES] = upper
    factor[:LANES, LANES:] = jnp.zeros_like(eye)
    factor[LANES:, LANES:] = lower
    factor[LANES:, :LANES] = -dot_exact(lower, dot_exact(across, upper, ((1,), (0,))), ((1,), (0,)))
    inverse = factor[...]
    lane = lax.broadcasted_iota(jnp.int32, (1, LANES), 1)
    parts = [corner[LANES - 4 + k:LANES - 3 + k, :] for k in range(4)]
    moved = jnp.concatenate(
        [jnp.where(lane < LANES // 2, parts[k], half_turn(parts[k + 1])) for k in (0, 2)], axis=1
    )
    halfway = jnp.sum(inverse * moved, axis=1, keepdims=True)
    mean_weight = jnp.sum(inverse * halfway, axis=0, keepdims=True)
    transform = (math.sqrt(prior) * inverse + mean_weight).astype(jnp.bfloat16)
    load.wait()
    widened = piece[...].astype(jnp.float32)
    state_mean = jnp.mean(widened, axis=1, keepdims=True)
    anomalies = (widened - state_mean).astype(jnp.bfloat16)
    change = lax.dot_general(anomalies, transform, (((1,), (1,)), ((), ())), preferred_element_type=jnp.float32)
    out_ref[...] = (state_mean + change).astype(jnp.bfloat16)


def analyse(sums, members, n_obs):
    slab_rows, width = members.shape
    rows = slab_rows // n_obs
    return pl.pallas_call(
        functools.partial(analyse_kernel, float(width - 1)),
        out_shape=jax.ShapeDtypeStruct((rows, width), jnp.bfloat16),
        in_specs=[VMEM, ANY],
        out_specs=VMEM,
        scratch_shapes=[
            pltpu.VMEM((rows, width), jnp.bfloat16),
            pltpu.VMEM((LANES, 2 * LANES), jnp.float32),
            pltpu.VMEM((LANES, 2 * LANES), jnp.float32),
            pltpu.VMEM((width, width), jnp.float32),
            pltpu.SemaphoreType.DMA,
        ],
        name="analyse",
    )(pltpu.with_memory_space_constraint(sums, pltpu.VMEM), members)


def on_device(n_obs, n_state, ensemble, obs_values, obs_error, h_blocks, block_rows, block_cols, block_count):
    members = ensemble[0]
    slab_rows, width = members.shape
    size = h_blocks.shape[-1]
    obs_blocks = obs_values.shape[0] // size
    sums = combine(
        members.reshape(slab_rows // size, size, width),
        h_blocks[0, 0],
        block_rows[0],
        block_cols[0],
        block_count,
        obs_values.reshape(obs_blocks, size),
        obs_error.reshape(obs_blocks, size),
        n_obs,
        n_state,
        obs_blocks,
    )
    return analyse(sums, members, n_obs)[None]


def solution(mesh):
    placed = (
        P("state", None, None),
        P("obs"),
        P("obs"),
        P("obs", "state", None, None, None),
        P("obs", "state", None),
        P("obs", "state", None),
        P("obs", "state"),
    )
    return jax.shard_map(
        functools.partial(on_device, mesh.shape["obs"], mesh.shape["state"]),
        mesh=mesh,
        in_specs=placed,
        out_specs=P("state", "obs", None),
        check_vma=False,
    )
```

```python
import functools
import math

import jax
import jax.numpy as jnp
from jax import lax
from jax.experimental import pallas as pl
from jax.experimental.pallas import tpu as pltpu
from jax.sharding import PartitionSpec as P

LANES = 128
SUBLANES = 8
BLOCKS = ((0, 0), (1, 0), (1, 1))
MESH = pl.DeviceIdType.MESH
VMEM = pl.BlockSpec(memory_space=pltpu.VMEM)
SMEM = pl.BlockSpec(memory_space=pltpu.SMEM)
ANY = pl.BlockSpec(memory_space=pl.ANY)
HIGHEST = lax.Precision.HIGHEST


def sort_slots(rows_row, live, obs_blocks, out):
    slots = rows_row.shape[1]
    at_row = lax.broadcasted_iota(jnp.int32, (1, slots), 1)
    key_row = jnp.where(at_row < live, rows_row, obs_blocks).astype(jnp.float32)
    sub = lax.broadcasted_iota(jnp.int32, (slots, slots), 0)
    lane = lax.broadcasted_iota(jnp.int32, (slots, slots), 1)
    keys = jnp.broadcast_to(key_row, (slots, slots))
    key_col = jnp.sum(jnp.where(sub == lane, keys, 0.0), axis=1, keepdims=True)
    ahead = (keys < key_col) | ((keys == key_col) & (lane < sub))
    rank = jnp.sum(jnp.where(ahead, 1.0, 0.0), axis=1, keepdims=True)
    place = lax.broadcasted_iota(jnp.int32, (slots, LANES), 1).astype(jnp.float32)
    slot = lax.broadcasted_iota(jnp.int32, (slots, LANES), 0).astype(jnp.float32)
    chosen = rank == place
    order = jnp.sum(jnp.where(chosen, slot, 0.0), axis=0, keepdims=True)
    sorted_key = jnp.sum(jnp.where(chosen, key_col, 0.0), axis=0, keepdims=True)
    smaller = jnp.sum(jnp.where(key_col < sorted_key, 1.0, 0.0), axis=0, keepdims=True)
    same = jnp.where(smaller == place[0:1], 0.0, 1.0)
    upto = jnp.sum(jnp.where(key_col <= place, 1.0, 0.0), axis=0, keepdims=True)
    present = jnp.sum(jnp.where(key_col == place, 1.0, 0.0), axis=0, keepdims=True)
    last = jnp.maximum(upto - 1.0, 0.0)
    out[0:1, :] = order.astype(jnp.int32)
    out[1:2, :] = same.astype(jnp.int32)
    out[2:3, :] = last.astype(jnp.int32)
    out[3:4, :] = jnp.minimum(present, 1.0).astype(jnp.int32)
    out[4:, :] = jnp.zeros_like(out[4:, :])


def project_half(half, lists, cols_ref, members, blocks, running, terms):
    slots = blocks.shape[0]
    together = math.gcd(slots, 16)

    def add_some(step, total):
        base = step * together
        products = []
        for k in range(together):
            slot = jnp.clip(lists[0, base + k], 0, slots - 1)
            picked = members[cols_ref[0, slot], :, half * LANES:(half + 1) * LANES]
            products.append(jnp.dot(blocks[slot], picked, preferred_element_type=jnp.float32))
        for k in range(together):
            total = total * lists[1, base + k].astype(jnp.float32) + products[k]
            running[base + k] = total
        return total

    lax.fori_loop(0, slots // together, add_some, jnp.zeros(running.shape[1:], jnp.float32))
    for row in range(terms.shape[1]):
        terms[half, row] = running[jnp.clip(lists[2, row], 0, slots - 1)] * lists[3, row].astype(jnp.float32)


def stage_plan(bits, order):
    plan = []
    for at, bit in enumerate(order):
        later = order[at + 1:]
        kept = [0]
        for other in later:
            kept = kept + [rel | (1 << other) for rel in kept]
        kept = sorted(kept, key=lambda rel: [-((rel >> other) & 1) for other in later])
        plan.append((bit, kept))
    return plan


def half_turn(row):
    return jnp.concatenate([row[:, LANES // 2:], row[:, :LANES // 2]], axis=1)


def columns_of(row):
    return jnp.transpose(jnp.broadcast_to(row, (LANES, LANES)))


def combine_kernel(n_obs, n_state, count_ref, cols_ref, rows_ref, members_hbm, blocks_hbm, values_ref, errors_ref, out_ref, members_in, blocks, sorted_in, lists, running, terms, loads, got0, got1, errs, innov, gram, part_in, mine, z_in, full, send, recv, send_b, recv_b):
    load_members = pltpu.make_async_copy(members_hbm, members_in, loads.at[0])
    load_blocks = pltpu.make_async_copy(blocks_hbm, blocks, loads.at[1])
    load_members.start()
    load_blocks.start()
    state = lax.axis_index("state")
    obs = lax.axis_index("obs")
    core = obs % 2
    z = obs // 2
    n_z = n_obs // 2
    bits = int(math.log2(n_state))
    group = n_state * 2
    share = errs.shape[0]
    members = 2 * terms.shape[3]
    per = share // LANES

    def flipped(rel):
        total = 0
        for bit in range(bits):
            own = (state // (1 << bit)) % 2
            total = total + (1 << bit) * ((own + ((rel >> bit) & 1)) % 2)
        return total

    far_first = sorted(range(1, group), key=lambda rel: -bin(rel // 2).count("1"))
    peer_index = [flipped(rel // 2) * 2 + (core + rel % 2) % 2 for rel in far_first]
    peers = [(z * 2 + index % 2, index // 2) for index in peer_index]
    z_peers = [(((z + shift) % n_z) * 2 + core, state) for shift in range(1, n_z)]

    barrier = pltpu.get_barrier_semaphore()
    for peer in peers + z_peers:
        pl.semaphore_signal(barrier, inc=1, device_id=peer, device_id_type=MESH)
    sort_slots(rows_ref[...], count_ref[0, 0], terms.shape[1], sorted_in)
    load_lists = pltpu.make_async_copy(sorted_in, lists, loads.at[2])
    load_lists.start()
    load_lists.wait()
    load_members.wait()
    load_blocks.wait()
    project_half(0, lists, cols_ref, members_in, blocks, running, terms)
    pl.semaphore_wait(barrier, len(peers) + len(z_peers))

    def piece(half, index):
        return terms.at[half, pl.ds(index * per, per)]

    got = (got0, got1)
    plans = (stage_plan(bits, list(range(bits))), stage_plan(bits, list(range(bits))[::-1]))
    slot_of = []
    for plan in plans:
        slots = {}
        for at, (bit, kept) in enumerate(plan):
            for rel in kept:
                slots[at, rel] = len(slots)
        slot_of.append(slots)
    copies = {}

    def launch(half, at, rel):
        bit = plans[half][at][0]
        sent_rel = rel | (1 << bit)
        if at == 0:
            source = piece(half, flipped(sent_rel))
        else:
            source = got[half].at[slot_of[half][at - 1, sent_rel]]
        slot = slot_of[half][at, rel]
        copy = pltpu.make_async_remote_copy(
            src_ref=source,
            dst_ref=got[half].at[slot],
            send_sem=send.at[half, slot],
            recv_sem=recv.at[half, slot],
            device_id=(obs, flipped(1 << bit)),
            device_id_type=MESH,
        )
        copy.start()
        copies[half, at, rel] = copy

    for half in range(2):
        if half == 1:
            project_half(1, lists, cols_ref, members_in, blocks, running, terms)
        for rel in plans[half][0][1]:
            launch(half, 0, rel)
    for k in range(per):
        at_rows = pl.ds(k * LANES, LANES)
        errs[at_rows] = 1.0 / columns_of(errors_ref[pl.ds(state * per + k, 1), :])
        innov[at_rows] = columns_of(values_ref[pl.ds(state * per + k, 1), :])
    for at in range(bits):
        for index in range(len(plans[0][at][1])):
            for half in range(2):
                rel = plans[half][at][1][index]
                copies[half, at, rel].wait_recv()
                slot = slot_of[half][at, rel]
                if at == 0:
                    got[half][slot] += terms[half, pl.ds(flipped(rel) * per, per)]
                else:
                    got[half][slot] += got[half][slot_of[half][at - 1, rel]]
                if at + 1 < bits and (rel >> plans[half][at + 1][0]) & 1:
                    launch(half, at + 1, rel ^ (1 << plans[half][at + 1][0]))
    last = [slot_of[half][bits - 1, 0] for half in range(2)]
    low, high = [got[half][last[half]].reshape(share, LANES) for half in range(2)]
    mean = (jnp.sum(low, axis=1, keepdims=True) + jnp.sum(high, axis=1, keepdims=True)) / members
    low = (low - mean) * errs[...]
    high = (high - mean) * errs[...]
    weight = (innov[...] - mean) * errs[...]
    sum_low = jnp.sum(low * weight, axis=0, keepdims=True)
    sum_high = jnp.sum(high * weight, axis=0, keepdims=True)
    whole = jnp.concatenate([low, high], axis=1)
    upper = whole.astype(jnp.bfloat16)
    rest = (whole - upper.astype(jnp.float32)).astype(jnp.bfloat16)
    turned = jnp.transpose(upper)
    square = jnp.dot(turned, upper, preferred_element_type=jnp.float32)
    cross = jnp.dot(turned, rest, preferred_element_type=jnp.float32)
    tiles = LANES // SUBLANES
    for k, (i, j) in enumerate(BLOCKS):
        block_i, block_j = slice(i * LANES, (i + 1) * LANES), slice(j * LANES, (j + 1) * LANES)
        block = square[block_i, block_j] + (cross[block_i, block_j] + jnp.transpose(cross[block_j, block_i]))
        gram[k * tiles:(k + 1) * tiles] = block.reshape(tiles, SUBLANES, LANES)
    lane = lax.broadcasted_iota(jnp.int32, (1, LANES), 1)
    for k, row in enumerate([sum_low, half_turn(sum_low), sum_high, half_turn(sum_high)]):
        at = SUBLANES - 4 + k
        gram[tiles - 1, at:at + 1, :] = jnp.where(lane < LANES // 2, row, gram[tiles - 1, at:at + 1, :])
    if gram.shape[0] > len(BLOCKS) * tiles:
        gram[len(BLOCKS) * tiles:] = jnp.zeros_like(gram[len(BLOCKS) * tiles:])

    own = state * 2 + core
    rows = gram.shape[0] // group

    def rows_of(index):
        return pl.ds(index * rows, rows)

    def send_to(source, target, at, peer):
        copy = pltpu.make_async_remote_copy(
            src_ref=source,
            dst_ref=target,
            send_sem=send_b.at[at],
            recv_sem=recv_b.at[at],
            device_id=peer,
            device_id_type=MESH,
        )
        copy.start()
        return copy

    first = []
    for k, peer in enumerate(peers):
        first.append(send_to(gram.at[rows_of(peer_index[k])], part_in.at[k], k, peer))
    total = gram[rows_of(own)]
    for k, copy in enumerate(first):
        copy.wait_recv()
        total = total + part_in[k]
    mine[...] = total
    second = []
    for k, peer in enumerate(z_peers):
        second.append(send_to(mine, z_in.at[k], group - 1 + k, peer))
    for k, copy in enumerate(second):
        copy.wait_recv()
        total = total + z_in[k]
    full[rows_of(own)] = total
    third = []
    for k, peer in enumerate(peers):
        third.append(send_to(full.at[rows_of(own)], full.at[rows_of(own)], group - 1 + n_z - 1 + k, peer))
    for copy in third:
        copy.wait_recv()
    out_ref[...] = full[...]
    for copy in list(copies.values()) + first + second + third:
        copy.wait_send()


def combine(members, blocks, rows, cols, count, values, errors, n_obs, n_state, obs_blocks):
    slots, size, unused = blocks.shape
    width = members.shape[-1]
    per = obs_blocks // n_state
    group = 2 * n_state
    n_z = n_obs // 2
    pieces = n_state - 1
    tiles = group * pl.cdiv(len(BLOCKS) * LANES // SUBLANES, group)
    others = 2 * (group - 1) + n_z - 1
    return pl.pallas_call(
        functools.partial(combine_kernel, n_obs, n_state),
        out_shape=pltpu.VMEM((tiles, SUBLANES, LANES), jnp.float32),
        in_specs=[SMEM, SMEM, VMEM, ANY, ANY, VMEM, VMEM],
        out_specs=VMEM,
        scratch_shapes=[
            pltpu.VMEM(members.shape, members.dtype),
            pltpu.VMEM(blocks.shape, blocks.dtype),
            pltpu.VMEM((SUBLANES, LANES), jnp.int32),
            pltpu.SMEM((SUBLANES, LANES), jnp.int32),
            pltpu.VMEM((slots, size, width // 2), jnp.float32),
            pltpu.VMEM((2, obs_blocks, size, width // 2), jnp.float32),
            pltpu.SemaphoreType.DMA((3,)),
            pltpu.VMEM((pieces, per, size, width // 2), jnp.float32),
            pltpu.VMEM((pieces, per, size, width // 2), jnp.float32),
            pltpu.VMEM((per * size, LANES), jnp.float32),
            pltpu.VMEM((per * size, LANES), jnp.float32),
            pltpu.VMEM((tiles, SUBLANES, LANES), jnp.float32),
            pltpu.VMEM((group - 1, tiles // group, SUBLANES, LANES), jnp.float32),
            pltpu.VMEM((tiles // group, SUBLANES, LANES), jnp.float32),
            pltpu.VMEM((n_z - 1, tiles // group, SUBLANES, LANES), jnp.float32),
            pltpu.VMEM((tiles, SUBLANES, LANES), jnp.float32),
            pltpu.SemaphoreType.DMA((2, pieces)),
            pltpu.SemaphoreType.DMA((2, pieces)),
            pltpu.SemaphoreType.DMA((others,)),
            pltpu.SemaphoreType.DMA((others,)),
        ],
        compiler_params=pltpu.CompilerParams(collective_id=0, has_side_effects=True),
        name="combine",
    )(count, cols, rows, members, blocks, values, errors)


def three_parts(x):
    first = x.astype(jnp.bfloat16)
    rest = x - first.astype(jnp.float32)
    second = rest.astype(jnp.bfloat16)
    third = (rest - second.astype(jnp.float32)).astype(jnp.bfloat16)
    return first, second, third


def inverse_factor(work):
    size = work.shape[0]
    step = 16
    lane = lax.broadcasted_iota(jnp.int32, (step, LANES), 1)
    sub = lax.broadcasted_iota(jnp.int32, (step, LANES), 0)
    row_of = lax.broadcasted_iota(jnp.int32, (size, 1), 0)

    def panel(at, carry):
        start = pl.multiple_of(at * step, step)
        left = work[pl.ds(start, step), :LANES]
        right = work[pl.ds(start, step), LANES:]
        cols = [
            jnp.broadcast_to(jnp.sum(jnp.where(lane == start + k, left, 0.0), axis=1, keepdims=True), (step, LANES))
            for k in range(step)
        ]
        for k in range(step):
            scale = lax.rsqrt(jnp.broadcast_to(cols[k][k:k + 1, :], (step, LANES)))
            factor = cols[k] * scale
            below = sub > k

            def eliminate(x):
                row = jnp.broadcast_to(x[k:k + 1, :], (step, LANES)) * scale
                return jnp.where(below, x - factor * row, jnp.where(sub == k, row, x))

            left = eliminate(left)
            right = eliminate(right)
            for m in range(k + 1, step):
                cols[m] = eliminate(cols[m])
        work[pl.ds(start, step), :LANES] = left
        work[pl.ds(start, step), LANES:] = right
        first, second, third = three_parts(left)
        wide = jnp.concatenate([left, right], axis=1)
        one, two, three = three_parts(wide)
        lhs = jnp.concatenate([first, first, second, second, first, third], axis=0)
        rhs = jnp.concatenate([one, two, one, two, three, one], axis=0)
        change = lax.dot_general(lhs, rhs, (((0,), (0,)), ((), ())), preferred_element_type=jnp.float32)
        work[...] = jnp.where(row_of >= start + step, work[...] - change, work[...])
        return carry

    lax.fori_loop(0, size // step, panel, 0)


def dot_exact(a, b, dims):
    return lax.dot_general(a, b, (dims, ((), ())), precision=HIGHEST, preferred_element_type=jnp.float32)


def analyse_kernel(prior, sums, members_hbm, out_ref, piece, first, second, factor, sem):
    rows, members = piece.shape
    load = pltpu.make_async_copy(members_hbm.at[pl.ds(lax.axis_index("obs") * rows, rows)], piece, sem)
    load.start()
    row_at = lax.broadcasted_iota(jnp.int32, (LANES, LANES), 0)
    col_at = lax.broadcasted_iota(jnp.int32, (LANES, LANES), 1)
    tiles = LANES // SUBLANES
    corner, side, other = [sums[k * tiles:(k + 1) * tiles].reshape(LANES, LANES) for k in range(len(BLOCKS))]
    eye = jnp.where(row_at == col_at, 1.0, 0.0).astype(jnp.float32)
    first[:, :LANES] = corner + prior * eye
    first[:, LANES:] = eye
    inverse_factor(first)
    upper = first[:, LANES:]
    across = dot_exact(side, upper, ((1,), (1,)))
    second[:, :LANES] = other + prior * eye - dot_exact(across, across, ((1,), (1,)))
    second[:, LANES:] = eye
    inverse_factor(second)
    lower = second[:, LANES:]
    factor[:LANES, :LANES] = upper
    factor[:LANES, LANES:] = jnp.zeros_like(eye)
    factor[LANES:, LANES:] = lower
    factor[LANES:, :LANES] = -dot_exact(lower, dot_exact(across, upper, ((1,), (0,))), ((1,), (0,)))
    inverse = factor[...]
    lane = lax.broadcasted_iota(jnp.int32, (1, LANES), 1)
    parts = [corner[LANES - 4 + k:LANES - 3 + k, :] for k in range(4)]
    moved = jnp.concatenate(
        [jnp.where(lane < LANES // 2, parts[k], half_turn(parts[k + 1])) for k in (0, 2)], axis=1
    )
    halfway = jnp.sum(inverse * moved, axis=1, keepdims=True)
    mean_weight = jnp.sum(inverse * halfway, axis=0, keepdims=True)
    transform = (math.sqrt(prior) * inverse + mean_weight).astype(jnp.bfloat16)
    load.wait()
    widened = piece[...].astype(jnp.float32)
    state_mean = jnp.mean(widened, axis=1, keepdims=True)
    anomalies = (widened - state_mean).astype(jnp.bfloat16)
    change = lax.dot_general(anomalies, transform, (((1,), (1,)), ((), ())), preferred_element_type=jnp.float32)
    out_ref[...] = (state_mean + change).astype(jnp.bfloat16)


def analyse(sums, members, n_obs):
    slab_rows, width = members.shape
    rows = slab_rows // n_obs
    return pl.pallas_call(
        functools.partial(analyse_kernel, float(width - 1)),
        out_shape=jax.ShapeDtypeStruct((rows, width), jnp.bfloat16),
        in_specs=[VMEM, ANY],
        out_specs=VMEM,
        scratch_shapes=[
            pltpu.VMEM((rows, width), jnp.bfloat16),
            pltpu.VMEM((LANES, 2 * LANES), jnp.float32),
            pltpu.VMEM((LANES, 2 * LANES), jnp.float32),
            pltpu.VMEM((width, width), jnp.float32),
            pltpu.SemaphoreType.DMA,
        ],
        name="analyse",
    )(pltpu.with_memory_space_constraint(sums, pltpu.VMEM), members)


def on_device(n_obs, n_state, ensemble, obs_values, obs_error, h_blocks, block_rows, block_cols, block_count):
    members = ensemble[0]
    slab_rows, width = members.shape
    size = h_blocks.shape[-1]
    obs_blocks = obs_values.shape[0] // size
    sums = combine(
        members.reshape(slab_rows // size, size, width),
        h_blocks[0, 0],
        block_rows[0],
        block_cols[0],
        block_count,
        obs_values.reshape(obs_blocks, size),
        obs_error.reshape(obs_blocks, size),
        n_obs,
        n_state,
        obs_blocks,
    )
    return analyse(sums, members, n_obs)[None]


def solution(mesh):
    placed = (
        P("state", None, None),
        P("obs"),
        P("obs"),
        P("obs", "state", None, None, None),
        P("obs", "state", None),
        P("obs", "state", None),
        P("obs", "state"),
    )
    return jax.shard_map(
        functools.partial(on_device, mesh.shape["obs"], mesh.shape["state"]),
        mesh=mesh,
        in_specs=placed,
        out_specs=P("state", "obs", None),
        check_vma=False,
    )
```
